32 devices in a mesh: runs: 2 (over x), tm: 16 (over z, y, core), pix: 1.
Axes of the slice: x: 2, y: 2, z: 4, core: 2. Of those that a mesh axis runs over, the one named last changes fastest.
Arguments:
- intensity: float32 [2048, 4096], P('tm', ('runs', 'pix')), parts along dimension 1, may hold values from 0.01 to 60
- cycle_label: int32 [4096], P(('runs', 'pix')), parts along dimension 0, may hold values from 0 to 127, as said below
- valid_mask: int32 [4096], P(('runs', 'pix')), parts along dimension 0, may hold values from 0 to 1, as said below
Outputs:
- correlation: float32 [128, 4096], P('tm', ('runs', 'pix')), parts along dimension 1
The draws below stay inside these ranges and needn't reach their ends.
There are 2 independent parts, one for each index of `runs`. The reference program is written for one: setup_inputs(seed, part) draws one part's arguments, and reference() takes and returns one part's arrays. A program takes and returns all parts, laid end to end along the dimension named above; each array names one. Nothing has to cross between parts.
Inputs may be any that keep to these rules, and one draw needn't show every extreme that they name: `cycle_label`: every cycle 0 to 127 is the label of exactly 16 pixels. `valid_mask`: every cycle holds at least one pixel marked 1.
All inputs are finite; a program needn't handle non-finite values.
Results may differ from the reference program's by a relative error of at most 0.0001.
Values sent between devices are 32-bit elements; how exact they have to be, the bound alone decides.
A program may use at most 64 MiB of HBM per device.

```python
import math
import jax
import jax.numpy as jnp
from jax import lax

Q = 128
LEVELS = 8
LAGS = 16
FRAMES = 2048
PIXELS = 2048


def pixel_layout(key):
    folded = jax.random.fold_in(key, 7)
    first_key, second_key = jax.random.split(folded)
    order = jax.random.permutation(first_key, PIXELS).astype(jnp.int32)
    draws_bits = jax.random.randint(second_key, (PIXELS,), 0, 16)
    labels = (order % Q).astype(jnp.int32)
    marked = jnp.where(order < Q, 1, jnp.where(draws_bits != 0, 1, 0)).astype(jnp.int32)
    return (labels, marked)


def draw_cycle_label(key, part):
    labels, marked = pixel_layout(key)
    return labels


def draw_valid_mask(key, part):
    labels, marked = pixel_layout(key)
    return marked


def draw_intensity(key, part):
    keys = jax.random.split(key, 4)
    position = jnp.arange(PIXELS, dtype=jnp.float32) / max(PIXELS - 1, 1)
    rough = jnp.exp(jax.random.uniform(keys[0], (PIXELS,), jnp.float32, math.log(0.5), math.log(2.0)))
    base = (1.0 + 2.0 * position) * rough
    flux = jnp.exp(jax.random.uniform(keys[1], (FRAMES,), jnp.float32, math.log(0.3), math.log(3.0)))
    noise = jax.random.normal(keys[3], (FRAMES, PIXELS), jnp.float32)
    rising = jnp.arange(FRAMES, dtype=jnp.float32) / max(FRAMES - 1, 1)
    contrast = 0.3 * (1.0 + 2.0 * rising)
    memory = jax.random.uniform(keys[2], (PIXELS,), jnp.float32, 0.3, 0.98)
    spread = jnp.sqrt(1.0 - memory * memory)

    def advance(carried, fresh):
        updated = memory * carried + spread * fresh
        return (updated, updated)
    unused, speckle = lax.scan(advance, jnp.zeros((PIXELS,), jnp.float32), noise)
    values = flux[:, None] * base[None, :] * (1.0 + contrast[:, None] * jnp.tanh(speckle))
    return values.astype(jnp.float32)


def setup_inputs(seed: int = 0, part: int = 0) -> dict:
    seeds = jax.random.split(jax.random.key(seed), 4)
    part_splits = jax.random.split(jax.random.fold_in(seeds[3], part), 4)
    intensity = draw_intensity(jax.random.fold_in(jax.random.fold_in(seeds[3], part), 71), part)
    cycle_label = draw_cycle_label(jax.random.fold_in(jax.random.fold_in(seeds[3], part), 71), part)
    valid_mask = draw_valid_mask(jax.random.fold_in(jax.random.fold_in(seeds[3], part), 71), part)
    return dict(intensity=intensity, cycle_label=cycle_label, valid_mask=valid_mask)


def coarsen(series):
    paired = series.reshape(series.shape[0] // 2, 2, series.shape[1])
    return (paired[:, 0] + paired[:, 1]) * 0.5


def level_rows(series, extension, total_frames):
    frames_here = series.shape[0]
    padded = jnp.concatenate([series, extension], axis=0)
    row_list = []
    for offset in range(extension.shape[0] + 1):
        product = series * padded[offset:offset + frames_here]
        row_list.append(jnp.sum(product, axis=0) / (total_frames - offset))
    return row_list


def normalize(intensity, cycle_label, valid_mask):
    valid_flag = valid_mask.astype(jnp.float32)
    member = (cycle_label[:, None] == jnp.arange(Q, dtype=jnp.int32)[None, :]).astype(jnp.float32)
    weighted = member * valid_flag[:, None]
    cycle_sum = jnp.dot(intensity, weighted, precision=lax.Precision.HIGHEST)
    cycle_count = jnp.sum(weighted, axis=0)
    cycle_mean = cycle_sum / cycle_count[None, :]
    per_pixel = jnp.dot(cycle_mean, member.T, precision=lax.Precision.HIGHEST)
    return valid_flag[None, :] * intensity / per_pixel


def reference(intensity, cycle_label, valid_mask):
    series = normalize(intensity, cycle_label, valid_mask)
    row_list = []
    for height in range(LEVELS):
        if height > 0:
            series = coarsen(series)
        extension = jnp.zeros((LAGS - 1, series.shape[1]), jnp.float32)
        row_list = row_list + level_rows(series, extension, series.shape[0])
    return jnp.stack(row_list)
```

```python
import functools
import jax
import jax.numpy as jnp
from jax import lax
from jax.experimental import pallas as pl
from jax.experimental.pallas import tpu as pltpu
from jax.sharding import PartitionSpec as P

Q = 128
LEVELS = 8
LAGS = 16


def coarsen(series):
    paired = series.reshape(series.shape[0] // 2, 2, series.shape[1])
    return (paired[:, 0] + paired[:, 1]) * 0.5


def level_rows(series, extension, total_frames):
    frames_here = series.shape[0]
    row_list = []
    for offset in range(extension.shape[0] + 1):
        inside = min(offset, frames_here)
        total = jnp.sum(series[: frames_here - inside] * series[inside:], axis=0)
        if offset > 0:
            tail_rows = series[frames_here - inside :]
            total = total + jnp.sum(tail_rows * extension[offset - inside : offset], axis=0)
        row_list.append(total / (total_frames - offset))
    return row_list


def pixel_rows(gathered):
    series = gathered[:, 0, :]
    row_list = []
    for height in range(LEVELS):
        if height > 0:
            series = coarsen(series)
        extension = jnp.zeros((LAGS - 1, series.shape[1]), jnp.float32)
        row_list = row_list + level_rows(series, extension, series.shape[0])
    return jnp.stack(row_list)


def body(intensity, cycle_label, valid_mask):
    valid_flag = valid_mask.astype(jnp.float32)
    member = (cycle_label[:, None] == jnp.arange(Q, dtype=jnp.int32)[None, :]).astype(jnp.float32)
    weighted = member * valid_flag[:, None]
    partial_sum = jnp.dot(intensity, weighted, precision=lax.Precision.HIGHEST)
    partial_count = jnp.sum(weighted, axis=0)
    cycle_sum, cycle_count = lax.psum((partial_sum, partial_count), "pix")
    cycle_mean = cycle_sum / cycle_count[None, :]
    per_pixel = lax.dot_general(
        cycle_mean, member, (((1,), (1,)), ((), ())), precision=lax.Precision.HIGHEST
    )
    normed = valid_flag[None, :] * intensity / per_pixel
    devices_tm = lax.axis_size("tm")
    tile_width = normed.shape[1] // devices_tm
    pieces = normed.reshape(normed.shape[0], devices_tm, tile_width)
    rows_local = pixel_rows(lax.all_to_all(pieces, "tm", split_axis=1, concat_axis=0, tiled=True))
    return lax.all_to_all(rows_local, "tm", split_axis=0, concat_axis=1, tiled=True)

LOCAL = 3
LANES = 128
SUB = 8


def split3(x):
    high = x.astype(jnp.bfloat16)
    rest = x - high.astype(jnp.float32)
    mid = rest.astype(jnp.bfloat16)
    low = (rest - mid.astype(jnp.float32)).astype(jnp.bfloat16)
    return high, mid, low


def fold_rows(parts):
    row = lax.broadcasted_iota(jnp.int32, (SUB, LANES), 0)
    for step in (4, 2, 1):
        keep = (row & step) == 0

        def swap(v, step=step, keep=keep):
            if step == 4:
                return pltpu.roll(v, 4, 0)
            return jnp.where(keep, pltpu.roll(v, SUB - step, 0), pltpu.roll(v, step, 0))

        parts = [
            jnp.where(keep, parts[i], parts[i + step]) + swap(jnp.where(keep, parts[i + step], parts[i]))
            for i in range(step)
        ]
    return parts[0]


def add_lags(ref, c, blocks, sums):
    for b in blocks:
        base = ref[c, pl.ds(b * SUB, SUB), :]
        for k in range(LAGS):
            term = base * ref[c, pl.ds(b * SUB + k, SUB), :]
            sums[k] = term if sums[k] is None else sums[k] + term
    return sums


def halve(ref, c, start, count):
    even = ref[c, pl.ds(start, count, stride=2), :]
    odd = ref[c, pl.ds(start + 1, count, stride=2), :]
    return (even + odd) * 0.5


def kernel(n, frames, x_hbm, lab_ref, val_ref, out_ref, *scratch):
    it = iter(scratch)
    x, wt = next(it), next(it)
    series = [next(it) for _ in range(LOCAL + 1)]
    far = [next(it) for _ in range(LEVELS - LOCAL)]
    keepers, partial, landed, result = next(it), next(it), next(it), next(it)
    load_sem, halo_send, halo_recv = next(it), next(it), next(it)
    a2a_send, a2a_recv, rs_send, rs_recv, out_send, out_recv = (next(it) for _ in range(6))
    me = lax.axis_index("tm")
    rows_out = LEVELS * LAGS // n
    total = n * frames
    groups = x.shape[1] // 256
    top = LOCAL * LAGS

    loads = [
        pltpu.make_async_copy(
            x_hbm.at[:, pl.ds(g * 256, 256)], x.at[:, pl.ds(g * 256, 256)], load_sem.at[g]
        )
        for g in range(groups)
    ]
    for copy in loads:
        copy.start()

    barrier = pltpu.get_barrier_semaphore()

    @pl.loop(1, n)
    def _(d):
        pl.semaphore_signal(
            barrier, inc=1, device_id={"tm": lax.rem(me + d, n)}, device_id_type=pl.DeviceIdType.MESH
        )

    cycle = lax.broadcasted_iota(jnp.int32, (Q, 256), 0)
    for g in range(groups):
        lab = lab_ref[:, pl.ds(g * 256, 256)]
        val = val_ref[:, pl.ds(g * 256, 256)].astype(jnp.float32)
        wt[g] = jnp.where(lab == cycle, val, 0.0).astype(jnp.bfloat16)
    ones = jnp.ones((16, 256), jnp.bfloat16)
    acc = jnp.zeros((3 * frames + 16, Q), jnp.float32)
    for g in range(groups):
        loads[g].wait()
        lhs = jnp.concatenate([*split3(x[:, pl.ds(g * 256, 256)]), ones], axis=0)
        acc = acc + lax.dot_general(
            lhs, wt[g], (((1,), (1,)), ((), ())), preferred_element_type=jnp.float32
        )
    cycle_sum = acc[:frames] + acc[frames : 2 * frames] + acc[2 * frames : 3 * frames]
    inverse = acc[3 * frames : 3 * frames + 1] / cycle_sum
    lhs = jnp.concatenate(split3(inverse), axis=0)
    for g in range(groups):
        parts = jnp.dot(lhs, wt[g], preferred_element_type=jnp.float32)
        scale = parts[:frames] + parts[frames : 2 * frames] + parts[2 * frames :]
        normed = x[:, pl.ds(g * 256, 256)] * scale
        series[0][2 * g, pl.ds(0, frames), :] = normed[:, :LANES]
        series[0][2 * g + 1, pl.ds(0, frames), :] = normed[:, LANES:]

    def coarse(c, carry):
        for l in range(1, LOCAL + 1):
            series[l][c, pl.ds(0, frames >> l), :] = halve(series[l - 1], c, 0, frames >> l)
        return carry

    lax.fori_loop(0, n, coarse, 0)

    pl.semaphore_wait(barrier, n - 1)

    def halo(l):
        first = 0 if l == 0 else SUB
        count = 2 * SUB - first
        return pltpu.make_async_remote_copy(
            src_ref=series[l].at[:, pl.ds(first, count), :],
            dst_ref=series[l].at[:, pl.ds((frames >> l) + first, count), :],
            send_sem=halo_send.at[l],
            recv_sem=halo_recv.at[l],
            device_id={"tm": lax.rem(me + n - 1, n)},
            device_id_type=pl.DeviceIdType.MESH,
        )

    @pl.when(me > 0)
    def _():
        for l in range(LOCAL):
            halo(l).start()

    @pl.when(me == n - 1)
    def _():
        for l in range(LOCAL):
            first = 0 if l == 0 else SUB
            series[l][:, pl.ds((frames >> l) + first, 2 * SUB - first), :] = jnp.zeros(
                (n, 2 * SUB - first, LANES), jnp.float32
            )

    deep = frames >> LOCAL

    def spread(peer, source):
        return pltpu.make_async_remote_copy(
            src_ref=series[LOCAL].at[peer],
            dst_ref=far[0].at[0, pl.ds(pl.multiple_of(source * deep, SUB), deep), :],
            send_sem=a2a_send.at[peer],
            recv_sem=a2a_recv.at[source],
            device_id={"tm": peer},
            device_id_type=pl.DeviceIdType.MESH,
        )

    @pl.loop(1, n)
    def _(d):
        spread(lax.rem(me + d, n), me).start()

    def inside(c, carry):
        for l in range(LOCAL):
            sums = add_lags(series[l], c, range((frames >> l) // SUB - 2), [None] * LAGS)
            for k in range(LAGS):
                keepers[c, l * LAGS + k] = sums[k]
        return carry

    lax.fori_loop(0, n, inside, 0)

    @pl.when(me < n - 1)
    def _():
        for l in range(LOCAL):
            halo(l).wait_recv()

    def reduce_to(peer, source):
        return pltpu.make_async_remote_copy(
            src_ref=partial.at[peer],
            dst_ref=landed.at[source],
            send_sem=rs_send.at[peer],
            recv_sem=rs_recv.at[source],
            device_id={"tm": peer},
            device_id_type=pl.DeviceIdType.MESH,
        )

    def edge(c):
        for l in range(LOCAL):
            here = frames >> l
            if l > 0:
                series[l][c, pl.ds(here, SUB), :] = halve(series[l - 1], c, 2 * here, SUB)
            sums = [keepers[c, l * LAGS + k] for k in range(LAGS)]
            sums = add_lags(series[l], c, range(here // SUB - 2, here // SUB), sums)
            for h in range(LAGS // SUB):
                partial[c, pl.ds(l * LAGS + h * SUB, SUB), :] = fold_rows(sums[h * SUB : (h + 1) * SUB])

    @pl.loop(1, n)
    def _(d):
        peer = lax.rem(me + d, n)
        edge(peer)
        reduce_to(peer, me).start()

    edge(me)

    far[0][0, pl.ds(pl.multiple_of(me * deep, SUB), deep), :] = series[LOCAL][me]
    for i in range(LEVELS - LOCAL):
        count = total >> (LOCAL + i)
        far[i][0, pl.ds(count, 2 * SUB), :] = jnp.zeros((2 * SUB, LANES), jnp.float32)

    @pl.loop(1, n)
    def _(d):
        spread(me, lax.rem(me + n - d, n)).wait_recv()

    lag = lax.broadcasted_iota(jnp.int32, (SUB, LANES), 0)

    def weight(l, h):
        return 1.0 / ((total >> l) - h * SUB - lag).astype(jnp.float32)

    for i in range(LEVELS - LOCAL):
        l = LOCAL + i
        count = total >> l
        if i > 0:
            far[i][0, pl.ds(0, count), :] = halve(far[i - 1], 0, 0, count)
        sums = add_lags(far[i], 0, range(count // SUB), [None] * LAGS)
        for h in range(LAGS // SUB):
            result[pl.ds(l * LAGS + h * SUB, SUB), :] = fold_rows(
                sums[h * SUB : (h + 1) * SUB]
            ) * weight(l, h)

    def deliver(peer, source):
        return pltpu.make_async_remote_copy(
            src_ref=result.at[pl.ds(pl.multiple_of(peer * rows_out, SUB), rows_out), :],
            dst_ref=out_ref.at[:, pl.ds(pl.multiple_of(source * LANES, LANES), LANES)],
            send_sem=out_send.at[peer],
            recv_sem=out_recv.at[source],
            device_id={"tm": peer},
            device_id_type=pl.DeviceIdType.MESH,
        )

    split = top // rows_out

    @pl.loop(0, n)
    def _(d):
        peer = lax.rem(me + d, n)

        @pl.when((peer >= split) & (peer != me))
        def _():
            deliver(peer, me).start()

    sums = [partial[me, pl.ds(r * SUB, SUB), :] for r in range(top // SUB)]

    def gather(d, sums):
        source = lax.rem(me + n - d, n)
        reduce_to(me, source).wait_recv()
        return tuple(s + landed[source, pl.ds(r * SUB, SUB), :] for r, s in enumerate(sums))

    sums = lax.fori_loop(1, n, gather, tuple(sums))
    for r in range(top // SUB):
        result[pl.ds(r * SUB, SUB), :] = sums[r] * weight(r * SUB // LAGS, r % (LAGS // SUB))

    @pl.loop(0, n)
    def _(d):
        peer = lax.rem(me + d, n)

        @pl.when((peer < split) & (peer != me))
        def _():
            deliver(peer, me).start()

    out_ref[:, pl.ds(pl.multiple_of(me * LANES, LANES), LANES)] = result[
        pl.ds(pl.multiple_of(me * rows_out, SUB), rows_out), :
    ]

    @pl.loop(1, n)
    def _(d):
        peer = lax.rem(me + d, n)
        deliver(me, lax.rem(me + n - d, n)).wait_recv()
        deliver(peer, me).wait_send()
        reduce_to(peer, me).wait_send()
        spread(peer, me).wait_send()

    @pl.when(me > 0)
    def _():
        for l in range(LOCAL):
            halo(l).wait_send()


def kernel_body(n, intensity, cycle_label, valid_mask):
    frames, pixels = intensity.shape
    f32 = jnp.float32
    dma = pltpu.SemaphoreType.DMA
    scratch = [
        pltpu.VMEM((frames, pixels), f32),
        pltpu.VMEM((pixels // 256, Q, 256), jnp.bfloat16),
    ]
    scratch += [pltpu.VMEM((n, (frames >> l) + 2 * SUB, LANES), f32) for l in range(LOCAL)]
    scratch += [pltpu.VMEM((n, frames >> LOCAL, LANES), f32)]
    scratch += [
        pltpu.VMEM((1, (n * frames >> l) + 2 * SUB, LANES), f32) for l in range(LOCAL, LEVELS)
    ]
    scratch += [
        pltpu.VMEM((n, LOCAL * LAGS, SUB, LANES), f32),
        pltpu.VMEM((n, LOCAL * LAGS, LANES), f32),
        pltpu.VMEM((n, LOCAL * LAGS, LANES), f32),
        pltpu.VMEM((LEVELS * LAGS, LANES), f32),
        dma((pixels // 256,)),
        dma((LOCAL,)),
        dma((LOCAL,)),
    ] + [dma((n,))] * 6
    vmem = pl.BlockSpec(memory_space=pltpu.VMEM)
    return pl.pallas_call(
        functools.partial(kernel, n, frames),
        out_shape=jax.ShapeDtypeStruct((LEVELS * LAGS // n, pixels), f32),
        in_specs=[pl.BlockSpec(memory_space=pl.ANY), vmem, vmem],
        out_specs=vmem,
        scratch_shapes=scratch,
        compiler_params=pltpu.CompilerParams(collective_id=0, has_side_effects=True),
        name="multitau",
    )(intensity, cycle_label.reshape(1, pixels), valid_mask.reshape(1, pixels))


def route(intensity, cycle_label, valid_mask):
    n = lax.axis_size("tm")
    frames, pixels = intensity.shape
    fits = (
        lax.axis_size("pix") == 1
        and pixels == n * LANES
        and frames == SUB << (LEVELS - 1 - LOCAL)
        and (LEVELS * LAGS) % (n * SUB) == 0
    )
    if fits:
        return kernel_body(n, intensity, cycle_label, valid_mask)
    return body(intensity, cycle_label, valid_mask)


def solution(mesh):
    placed = (P("tm", ("runs", "pix")), P(("runs", "pix")), P(("runs", "pix")))
    return jax.shard_map(
        route, mesh=mesh, in_specs=placed, out_specs=P("tm", ("runs", "pix")), check_vma=False
    )
```

```python
import functools
import jax
import jax.numpy as jnp
from jax import lax
from jax.experimental import pallas as pl
from jax.experimental.pallas import tpu as pltpu
from jax.sharding import PartitionSpec as P

Q = 128
LEVELS = 8
LAGS = 16


def coarsen(series):
    paired = series.reshape(series.shape[0] // 2, 2, series.shape[1])
    return (paired[:, 0] + paired[:, 1]) * 0.5


def level_rows(series, extension, total_frames):
    frames_here = series.shape[0]
    row_list = []
    for offset in range(extension.shape[0] + 1):
        inside = min(offset, frames_here)
        total = jnp.sum(series[: frames_here - inside] * series[inside:], axis=0)
        if offset > 0:
            tail_rows = series[frames_here - inside :]
            total = total + jnp.sum(tail_rows * extension[offset - inside : offset], axis=0)
        row_list.append(total / (total_frames - offset))
    return row_list


def pixel_rows(gathered):
    series = gathered[:, 0, :]
    row_list = []
    for height in range(LEVELS):
        if height > 0:
            series = coarsen(series)
        extension = jnp.zeros((LAGS - 1, series.shape[1]), jnp.float32)
        row_list = row_list + level_rows(series, extension, series.shape[0])
    return jnp.stack(row_list)


def body(intensity, cycle_label, valid_mask):
    valid_flag = valid_mask.astype(jnp.float32)
    member = (cycle_label[:, None] == jnp.arange(Q, dtype=jnp.int32)[None, :]).astype(jnp.float32)
    weighted = member * valid_flag[:, None]
    partial_sum = jnp.dot(intensity, weighted, precision=lax.Precision.HIGHEST)
    partial_count = jnp.sum(weighted, axis=0)
    cycle_sum, cycle_count = lax.psum((partial_sum, partial_count), "pix")
    cycle_mean = cycle_sum / cycle_count[None, :]
    per_pixel = lax.dot_general(
        cycle_mean, member, (((1,), (1,)), ((), ())), precision=lax.Precision.HIGHEST
    )
    normed = valid_flag[None, :] * intensity / per_pixel
    devices_tm = lax.axis_size("tm")
    tile_width = normed.shape[1] // devices_tm
    pieces = normed.reshape(normed.shape[0], devices_tm, tile_width)
    rows_local = pixel_rows(lax.all_to_all(pieces, "tm", split_axis=1, concat_axis=0, tiled=True))
    return lax.all_to_all(rows_local, "tm", split_axis=0, concat_axis=1, tiled=True)

LOCAL = 2
CHUNKS = 4
LANES = 128
SUB = 8


def split3(x):
    high = x.astype(jnp.bfloat16)
    rest = x - high.astype(jnp.float32)
    mid = rest.astype(jnp.bfloat16)
    low = (rest - mid.astype(jnp.float32)).astype(jnp.bfloat16)
    return high, mid, low


def fold_rows(parts):
    row = lax.broadcasted_iota(jnp.int32, (SUB, LANES), 0)
    for step in (4, 2, 1):
        keep = (row & step) == 0

        def swap(v, step=step, keep=keep):
            if step == 4:
                return pltpu.roll(v, 4, 0)
            return jnp.where(keep, pltpu.roll(v, SUB - step, 0), pltpu.roll(v, step, 0))

        parts = [
            jnp.where(keep, parts[i], parts[i + step]) + swap(jnp.where(keep, parts[i + step], parts[i]))
            for i in range(step)
        ]
    return parts[0]


def add_lags(ref, c, blocks, sums):
    for b in blocks:
        base = ref[c, pl.ds(b * SUB, SUB), :]
        for k in range(LAGS):
            term = base * ref[c, pl.ds(b * SUB + k, SUB), :]
            sums[k] = term if sums[k] is None else sums[k] + term
    return sums


def halve(ref, c, start, count):
    even = ref[c, pl.ds(start, count, stride=2), :]
    odd = ref[c, pl.ds(start + 1, count, stride=2), :]
    return (even + odd) * 0.5


def kernel(n, frames, x_hbm, lab_ref, val_ref, out_ref, *scratch):
    it = iter(scratch)
    x, wt = next(it), next(it)
    series = [next(it) for _ in range(LOCAL + 1)]
    far = [next(it) for _ in range(LEVELS - LOCAL)]
    keepers, partial, inbox0, inbox, result = (next(it) for _ in range(5))
    load_sem, halo_send, halo_recv = next(it), next(it), next(it)
    hop_send, hop_recv, a2a_send, a2a_recv, out_send, out_recv = (next(it) for _ in range(6))
    me = lax.axis_index("tm")
    rows_out = LEVELS * LAGS // n
    total = n * frames
    groups = x.shape[1] // 256
    keep = LOCAL * LAGS // rows_out

    loads = [
        pltpu.make_async_copy(
            x_hbm.at[:, pl.ds(g * 256, 256)], x.at[:, pl.ds(g * 256, 256)], load_sem.at[g]
        )
        for g in range(groups)
    ]
    for copy in loads:
        copy.start()

    barrier = pltpu.get_barrier_semaphore()

    @pl.loop(1, n)
    def _(d):
        pl.semaphore_signal(
            barrier, inc=1, device_id={"tm": lax.rem(me + d, n)}, device_id_type=pl.DeviceIdType.MESH
        )

    cycle = lax.broadcasted_iota(jnp.int32, (Q, 256), 0)
    for g in range(groups):
        lab = lab_ref[:, pl.ds(g * 256, 256)]
        val = val_ref[:, pl.ds(g * 256, 256)].astype(jnp.float32)
        wt[g] = jnp.where(lab == cycle, val, 0.0).astype(jnp.bfloat16)
    ones = jnp.ones((16, 256), jnp.bfloat16)
    acc = jnp.zeros((3 * frames + 16, Q), jnp.float32)
    for g in range(groups):
        loads[g].wait()
        lhs = jnp.concatenate([*split3(x[:, pl.ds(g * 256, 256)]), ones], axis=0)
        acc = acc + lax.dot_general(
            lhs, wt[g], (((1,), (1,)), ((), ())), preferred_element_type=jnp.float32
        )
    cycle_sum = acc[:frames] + acc[frames : 2 * frames] + acc[2 * frames : 3 * frames]
    inverse = acc[3 * frames : 3 * frames + 1] / cycle_sum
    lhs = jnp.concatenate(split3(inverse), axis=0)
    for g in range(groups):
        parts = jnp.dot(lhs, wt[g], preferred_element_type=jnp.float32)
        scale = parts[:frames] + parts[frames : 2 * frames] + parts[2 * frames :]
        normed = x[:, pl.ds(g * 256, 256)] * scale
        series[0][2 * g, pl.ds(0, frames), :] = normed[:, :LANES]
        series[0][2 * g + 1, pl.ds(0, frames), :] = normed[:, LANES:]

    def coarse(c, carry):
        for l in range(1, LOCAL + 1):
            series[l][c, pl.ds(0, frames >> l), :] = halve(series[l - 1], c, 0, frames >> l)
        return carry

    lax.fori_loop(0, n, coarse, 0)

    pl.semaphore_wait(barrier, n - 1)

    def halo(l):
        first = 0 if l == 0 else SUB
        count = 2 * SUB - first
        return pltpu.make_async_remote_copy(
            src_ref=series[l].at[:, pl.ds(first, count), :],
            dst_ref=series[l].at[:, pl.ds((frames >> l) + first, count), :],
            send_sem=halo_send.at[l],
            recv_sem=halo_recv.at[l],
            device_id={"tm": lax.rem(me + n - 1, n)},
            device_id_type=pl.DeviceIdType.MESH,
        )

    @pl.when(me > 0)
    def _():
        for l in range(LOCAL):
            halo(l).start()

    @pl.when(me == n - 1)
    def _():
        for l in range(LOCAL):
            first = 0 if l == 0 else SUB
            series[l][:, pl.ds((frames >> l) + first, 2 * SUB - first), :] = jnp.zeros(
                (n, 2 * SUB - first, LANES), jnp.float32
            )

    deep = frames >> LOCAL

    def spread(peer, source):
        return pltpu.make_async_remote_copy(
            src_ref=series[LOCAL].at[peer],
            dst_ref=far[0].at[0, pl.ds(pl.multiple_of(source * deep, SUB), deep), :],
            send_sem=a2a_send.at[peer],
            recv_sem=a2a_recv.at[source],
            device_id={"tm": peer},
            device_id_type=pl.DeviceIdType.MESH,
        )

    @pl.loop(1, n)
    def _(d):
        spread(lax.rem(me + n - d, n), me).start()

    def inside(c, carry):
        for l in range(LOCAL):
            sums = add_lags(series[l], c, range((frames >> l) // SUB - 2), [None] * LAGS)
            for k in range(LAGS):
                keepers[c, l * LAGS + k] = sums[k]
        return carry

    lax.fori_loop(0, n, inside, 0)

    @pl.when(me < n - 1)
    def _():
        for l in range(LOCAL):
            halo(l).wait_recv()

    side, level = lax.rem(me, 2), lax.rem(me // 2, 2)
    block = n // CHUNKS
    stages = [1, 2]
    while 2 * stages[-1] < n:
        stages.append(2 * stages[-1])

    def hop(s, q):
        b = stages[s]
        part = pl.ds(q * block, block)
        if s == 0:
            src, dst = partial.at[1 - side, :, part], inbox0.at[:, part]
        elif s == 1:
            src, dst = partial.at[side, 1 - level, part], inbox.at[0, part]
        else:
            src, dst = partial.at[side, level, part], inbox.at[s - 1, part]
        target = me + b - 2 * b * lax.rem(me // b, 2) if s < 2 else lax.rem(me + n - b, n)
        return pltpu.make_async_remote_copy(
            src_ref=src,
            dst_ref=dst,
            send_sem=hop_send.at[s, q],
            recv_sem=hop_recv.at[s, q],
            device_id={"tm": target},
            device_id_type=pl.DeviceIdType.MESH,
        )

    def sends(s):
        b = stages[s]
        return (lax.rem(me, 2 * b) >= b) & (lax.rem(me, b) < 4)

    def receives(s):
        return lax.rem(me, 2 * stages[s]) < 4

    def edge(c, carry):
        for l in range(LOCAL):
            here = frames >> l
            if l > 0:
                series[l][c, pl.ds(here, SUB), :] = halve(series[l - 1], c, 2 * here, SUB)
            sums = [keepers[c, l * LAGS + k] for k in range(LAGS)]
            sums = add_lags(series[l], c, range(here // SUB - 2, here // SUB), sums)
            for h in range(LAGS // SUB):
                partial[h, l, c] = fold_rows(sums[h * SUB : (h + 1) * SUB])
        return carry

    for q in range(CHUNKS):
        lax.fori_loop(q * block, (q + 1) * block, edge, 0)
        hop(0, q).start()
    for q in range(CHUNKS):
        part = pl.ds(q * block, block)
        hop(0, q).wait_recv()
        partial[side, :, part] = partial[side, :, part] + inbox0[:, part]
        hop(1, q).start()
    for q in range(CHUNKS):
        part = pl.ds(q * block, block)
        hop(1, q).wait_recv()
        partial[side, level, part] = partial[side, level, part] + inbox[0, part]

        @pl.when(sends(2))
        def _():
            hop(2, q).start()

    far[0][0, pl.ds(pl.multiple_of(me * deep, SUB), deep), :] = series[LOCAL][me]
    for i in range(LEVELS - LOCAL):
        count = total >> (LOCAL + i)
        far[i][0, pl.ds(count, 2 * SUB), :] = jnp.zeros((2 * SUB, LANES), jnp.float32)

    @pl.loop(1, n)
    def _(d):
        spread(me, lax.rem(me + n - d, n)).wait_recv()

    lag = lax.broadcasted_iota(jnp.int32, (SUB, LANES), 0)

    def weight(l, h):
        return 1.0 / ((total >> l) - h * SUB - lag).astype(jnp.float32)

    for i in range(LEVELS - LOCAL):
        l = LOCAL + i
        count = total >> l
        if i > 0:
            far[i][0, pl.ds(0, count), :] = halve(far[i - 1], 0, 0, count)
        sums = add_lags(far[i], 0, range(count // SUB), [None] * LAGS)
        for h in range(LAGS // SUB):
            result[pl.ds(l * LAGS + h * SUB, SUB), :] = fold_rows(
                sums[h * SUB : (h + 1) * SUB]
            ) * weight(l, h)

    def deliver(peer, source):
        return pltpu.make_async_remote_copy(
            src_ref=result.at[pl.ds(pl.multiple_of(peer * rows_out, SUB), rows_out), :],
            dst_ref=out_ref.at[:, pl.ds(pl.multiple_of(source * LANES, LANES), LANES)],
            send_sem=out_send.at[peer],
            recv_sem=out_recv.at[source],
            device_id={"tm": peer},
            device_id_type=pl.DeviceIdType.MESH,
        )

    @pl.loop(1, n)
    def _(d):
        peer = lax.rem(me + n - d, n)

        @pl.when(peer >= keep)
        def _():
            deliver(peer, me).start()

    for s in range(2, len(stages)):

        @pl.when(receives(s))
        def _():
            for q in range(CHUNKS):
                part = pl.ds(q * block, block)
                hop(s, q).wait_recv()
                partial[side, level, part] = partial[side, level, part] + inbox[s - 1, part]
                if s + 1 < len(stages):

                    @pl.when(sends(s + 1))
                    def _():
                        hop(s + 1, q).start()

    @pl.when(me < keep)
    def _():
        count = total // (level + 1) - side * SUB
        scale = 1.0 / (count - lag).astype(jnp.float32)
        for c in range(n):
            out_ref[:, pl.ds(c * LANES, LANES)] = partial[side, level, c] * scale

    @pl.when(me >= keep)
    def _():
        out_ref[:, pl.ds(pl.multiple_of(me * LANES, LANES), LANES)] = result[
            pl.ds(pl.multiple_of(me * rows_out, SUB), rows_out), :
        ]

        @pl.loop(1, n)
        def _(d):
            deliver(me, lax.rem(me + n - d, n)).wait_recv()

    @pl.loop(1, n)
    def _(d):
        peer = lax.rem(me + n - d, n)
        spread(peer, me).wait_send()

        @pl.when(peer >= keep)
        def _():
            deliver(peer, me).wait_send()

    for q in range(CHUNKS):
        hop(0, q).wait_send()
        hop(1, q).wait_send()
    for s in range(2, len(stages)):

        @pl.when(sends(s))
        def _():
            for q in range(CHUNKS):
                hop(s, q).wait_send()

    @pl.when(me > 0)
    def _():
        for l in range(LOCAL):
            halo(l).wait_send()


def kernel_body(n, intensity, cycle_label, valid_mask):
    frames, pixels = intensity.shape
    f32 = jnp.float32
    dma = pltpu.SemaphoreType.DMA
    scratch = [
        pltpu.VMEM((frames, pixels), f32),
        pltpu.VMEM((pixels // 256, Q, 256), jnp.bfloat16),
    ]
    scratch += [pltpu.VMEM((n, (frames >> l) + 2 * SUB, LANES), f32) for l in range(LOCAL)]
    scratch += [pltpu.VMEM((n, frames >> LOCAL, LANES), f32)]
    scratch += [
        pltpu.VMEM((1, (n * frames >> l) + 2 * SUB, LANES), f32) for l in range(LOCAL, LEVELS)
    ]
    scratch += [
        pltpu.VMEM((n, LOCAL * LAGS, SUB, LANES), f32),
        pltpu.VMEM((2, 2, n, SUB, LANES), f32),
        pltpu.VMEM((2, n, SUB, LANES), f32),
        pltpu.VMEM((n.bit_length() - 2, n, SUB, LANES), f32),
        pltpu.VMEM((LEVELS * LAGS, LANES), f32),
        dma((pixels // 256,)),
        dma((LOCAL,)),
        dma((LOCAL,)),
        dma((n.bit_length() - 1, CHUNKS)),
        dma((n.bit_length() - 1, CHUNKS)),
    ] + [dma((n,))] * 4
    vmem = pl.BlockSpec(memory_space=pltpu.VMEM)
    return pl.pallas_call(
        functools.partial(kernel, n, frames),
        out_shape=jax.ShapeDtypeStruct((LEVELS * LAGS // n, pixels), f32),
        in_specs=[pl.BlockSpec(memory_space=pl.ANY), vmem, vmem],
        out_specs=vmem,
        scratch_shapes=scratch,
        compiler_params=pltpu.CompilerParams(collective_id=0, has_side_effects=True),
        name="multitau",
    )(intensity, cycle_label.reshape(1, pixels), valid_mask.reshape(1, pixels))


def route(intensity, cycle_label, valid_mask):
    n = lax.axis_size("tm")
    frames, pixels = intensity.shape
    fits = (
        lax.axis_size("pix") == 1
        and pixels == n * LANES
        and frames % (SUB << LOCAL) == 0
        and frames >> LOCAL >= 2 * SUB
        and LEVELS * LAGS == n * SUB
    )
    if fits:
        return kernel_body(n, intensity, cycle_label, valid_mask)
    return body(intensity, cycle_label, valid_mask)


def solution(mesh):
    placed = (P("tm", ("runs", "pix")), P(("runs", "pix")), P(("runs", "pix")))
    return jax.shard_map(
        route, mesh=mesh, in_specs=placed, out_specs=P("tm", ("runs", "pix")), check_vma=False
    )
```

```python
import functools
import jax
import jax.numpy as jnp
from jax import lax
from jax.experimental import pallas as pl
from jax.experimental.pallas import tpu as pltpu
from jax.sharding import PartitionSpec as P

Q = 128
LEVELS = 8
LAGS = 16


def coarsen(series):
    paired = series.reshape(series.shape[0] // 2, 2, series.shape[1])
    return (paired[:, 0] + paired[:, 1]) * 0.5


def level_rows(series, extension, total_frames):
    frames_here = series.shape[0]
    row_list = []
    for offset in range(extension.shape[0] + 1):
        inside = min(offset, frames_here)
        total = jnp.sum(series[: frames_here - inside] * series[inside:], axis=0)
        if offset > 0:
            tail_rows = series[frames_here - inside :]
            total = total + jnp.sum(tail_rows * extension[offset - inside : offset], axis=0)
        row_list.append(total / (total_frames - offset))
    return row_list


def pixel_rows(gathered):
    series = gathered[:, 0, :]
    row_list = []
    for height in range(LEVELS):
        if height > 0:
            series = coarsen(series)
        extension = jnp.zeros((LAGS - 1, series.shape[1]), jnp.float32)
        row_list = row_list + level_rows(series, extension, series.shape[0])
    return jnp.stack(row_list)


def body(intensity, cycle_label, valid_mask):
    valid_flag = valid_mask.astype(jnp.float32)
    member = (cycle_label[:, None] == jnp.arange(Q, dtype=jnp.int32)[None, :]).astype(jnp.float32)
    weighted = member * valid_flag[:, None]
    partial_sum = jnp.dot(intensity, weighted, precision=lax.Precision.HIGHEST)
    partial_count = jnp.sum(weighted, axis=0)
    cycle_sum, cycle_count = lax.psum((partial_sum, partial_count), "pix")
    cycle_mean = cycle_sum / cycle_count[None, :]
    per_pixel = lax.dot_general(
        cycle_mean, member, (((1,), (1,)), ((), ())), precision=lax.Precision.HIGHEST
    )
    normed = valid_flag[None, :] * intensity / per_pixel
    devices_tm = lax.axis_size("tm")
    tile_width = normed.shape[1] // devices_tm
    pieces = normed.reshape(normed.shape[0], devices_tm, tile_width)
    rows_local = pixel_rows(lax.all_to_all(pieces, "tm", split_axis=1, concat_axis=0, tiled=True))
    return lax.all_to_all(rows_local, "tm", split_axis=0, concat_axis=1, tiled=True)

LOCAL = 2
CHUNKS = 4
LANES = 128
SUB = 8


def split3(x):
    high = x.astype(jnp.bfloat16)
    rest = x - high.astype(jnp.float32)
    mid = rest.astype(jnp.bfloat16)
    low = (rest - mid.astype(jnp.float32)).astype(jnp.bfloat16)
    return high, mid, low


def fold_rows(parts):
    row = lax.broadcasted_iota(jnp.int32, (SUB, LANES), 0)
    for step in (4, 2, 1):
        keep = (row & step) == 0

        def swap(v, step=step, keep=keep):
            if step == 4:
                return pltpu.roll(v, 4, 0)
            return jnp.where(keep, pltpu.roll(v, SUB - step, 0), pltpu.roll(v, step, 0))

        parts = [
            jnp.where(keep, parts[i], parts[i + step]) + swap(jnp.where(keep, parts[i + step], parts[i]))
            for i in range(step)
        ]
    return parts[0]


def add_lags(ref, c, blocks, sums):
    for b in blocks:
        base = ref[c, pl.ds(b * SUB, SUB), :]
        for k in range(LAGS):
            term = base * ref[c, pl.ds(b * SUB + k, SUB), :]
            sums[k] = term if sums[k] is None else sums[k] + term
    return sums


def halve(ref, c, start, count):
    even = ref[c, pl.ds(start, count, stride=2), :]
    odd = ref[c, pl.ds(start + 1, count, stride=2), :]
    return (even + odd) * 0.5


def kernel(n, frames, x_hbm, lab_ref, val_ref, out_ref, *scratch):
    it = iter(scratch)
    x, wt = next(it), next(it)
    series = [next(it) for _ in range(LOCAL + 1)]
    far = [next(it) for _ in range(LEVELS - LOCAL)]
    keepers, partial, inbox0, inbox, result = (next(it) for _ in range(5))
    load_sem, halo_send, halo_recv = next(it), next(it), next(it)
    hop_send, hop_recv, a2a_send, a2a_recv, out_send, out_recv = (next(it) for _ in range(6))
    me = lax.axis_index("tm")
    rows_out = LEVELS * LAGS // n
    total = n * frames
    groups = x.shape[1] // 256
    keep = LOCAL * LAGS // rows_out

    loads = [
        pltpu.make_async_copy(
            x_hbm.at[:, pl.ds(g * 256, 256)], x.at[:, pl.ds(g * 256, 256)], load_sem.at[g]
        )
        for g in range(groups)
    ]
    for copy in loads:
        copy.start()

    barrier = pltpu.get_barrier_semaphore()

    @pl.loop(1, n)
    def _(d):
        pl.semaphore_signal(
            barrier, inc=1, device_id={"tm": lax.rem(me + d, n)}, device_id_type=pl.DeviceIdType.MESH
        )

    cycle = lax.broadcasted_iota(jnp.int32, (Q, 256), 0)
    for g in range(groups):
        lab = lab_ref[:, pl.ds(g * 256, 256)]
        val = val_ref[:, pl.ds(g * 256, 256)].astype(jnp.float32)
        wt[g] = jnp.where(lab == cycle, val, 0.0).astype(jnp.bfloat16)
    ones = jnp.ones((16, 256), jnp.bfloat16)
    acc = jnp.zeros((3 * frames + 16, Q), jnp.float32)
    for g in range(groups):
        loads[g].wait()
        lhs = jnp.concatenate([*split3(x[:, pl.ds(g * 256, 256)]), ones], axis=0)
        acc = acc + lax.dot_general(
            lhs, wt[g], (((1,), (1,)), ((), ())), preferred_element_type=jnp.float32
        )
    cycle_sum = acc[:frames] + acc[frames : 2 * frames] + acc[2 * frames : 3 * frames]
    inverse = acc[3 * frames : 3 * frames + 1] / cycle_sum
    lhs = jnp.concatenate(split3(inverse), axis=0)
    for g in range(groups):
        parts = jnp.dot(lhs, wt[g], preferred_element_type=jnp.float32)
        scale = parts[:frames] + parts[frames : 2 * frames] + parts[2 * frames :]
        normed = x[:, pl.ds(g * 256, 256)] * scale
        series[0][2 * g, pl.ds(0, frames), :] = normed[:, :LANES]
        series[0][2 * g + 1, pl.ds(0, frames), :] = normed[:, LANES:]

    def coarse(c, carry):
        for l in range(1, LOCAL + 1):
            series[l][c, pl.ds(0, frames >> l), :] = halve(series[l - 1], c, 0, frames >> l)
        return carry

    lax.fori_loop(0, n, coarse, 0)

    pl.semaphore_wait(barrier, n - 1)

    block = n // CHUNKS

    def halo(l, q):
        first = 0 if l == 0 else SUB
        count = 2 * SUB - first
        return pltpu.make_async_remote_copy(
            src_ref=series[l].at[pl.ds(q * block, block), pl.ds(first, count), :],
            dst_ref=series[l].at[pl.ds(q * block, block), pl.ds((frames >> l) + first, count), :],
            send_sem=halo_send.at[l, q],
            recv_sem=halo_recv.at[l, q],
            device_id={"tm": lax.rem(me + n - 1, n)},
            device_id_type=pl.DeviceIdType.MESH,
        )

    @pl.when(me > 0)
    def _():
        for q in range(CHUNKS):
            for l in range(LOCAL):
                halo(l, q).start()

    @pl.when(me == n - 1)
    def _():
        for l in range(LOCAL):
            first = 0 if l == 0 else SUB
            series[l][:, pl.ds((frames >> l) + first, 2 * SUB - first), :] = jnp.zeros(
                (n, 2 * SUB - first, LANES), jnp.float32
            )

    deep = frames >> LOCAL

    def spread(peer, source):
        return pltpu.make_async_remote_copy(
            src_ref=series[LOCAL].at[peer],
            dst_ref=far[0].at[0, pl.ds(pl.multiple_of(source * deep, SUB), deep), :],
            send_sem=a2a_send.at[peer],
            recv_sem=a2a_recv.at[source],
            device_id={"tm": peer},
            device_id_type=pl.DeviceIdType.MESH,
        )

    @pl.loop(1, n)
    def _(d):
        spread(lax.rem(me + d, n), me).start()

    def inside(c, carry):
        for l in range(LOCAL):
            sums = add_lags(series[l], c, range((frames >> l) // SUB - 2), [None] * LAGS)
            for k in range(LAGS):
                keepers[c, l * LAGS + k] = sums[k]
        return carry

    lax.fori_loop(0, n, inside, 0)

    side, level = lax.rem(me, 2), lax.rem(me // 2, 2)
    stages = [1, 2]
    while 2 * stages[-1] < n:
        stages.append(2 * stages[-1])

    def hop(s, q):
        b = stages[s]
        part = pl.ds(q * block, block)
        if s == 0:
            src, dst = partial.at[1 - side, :, part], inbox0.at[:, part]
        elif s == 1:
            src, dst = partial.at[side, 1 - level, part], inbox.at[0, part]
        else:
            src, dst = partial.at[side, level, part], inbox.at[s - 1, part]
        target = me + b - 2 * b * lax.rem(me // b, 2) if s < 2 else lax.rem(me + n - b, n)
        return pltpu.make_async_remote_copy(
            src_ref=src,
            dst_ref=dst,
            send_sem=hop_send.at[s, q],
            recv_sem=hop_recv.at[s, q],
            device_id={"tm": target},
            device_id_type=pl.DeviceIdType.MESH,
        )

    def sends(s):
        b = stages[s]
        return (lax.rem(me, 2 * b) >= b) & (lax.rem(me, b) < 4)

    def receives(s):
        return lax.rem(me, 2 * stages[s]) < 4

    def edge(c, carry):
        for l in range(LOCAL):
            here = frames >> l
            if l > 0:
                series[l][c, pl.ds(here, SUB), :] = halve(series[l - 1], c, 2 * here, SUB)
            sums = [keepers[c, l * LAGS + k] for k in range(LAGS)]
            sums = add_lags(series[l], c, range(here // SUB - 2, here // SUB), sums)
            for h in range(LAGS // SUB):
                partial[h, l, c] = fold_rows(sums[h * SUB : (h + 1) * SUB])
        return carry

    for q in range(CHUNKS):

        @pl.when(me < n - 1)
        def _():
            for l in range(LOCAL):
                halo(l, q).wait_recv()

        lax.fori_loop(q * block, (q + 1) * block, edge, 0)
        hop(0, q).start()
    for q in range(CHUNKS):
        part = pl.ds(q * block, block)
        hop(0, q).wait_recv()
        partial[side, :, part] = partial[side, :, part] + inbox0[:, part]
        hop(1, q).start()
    for q in range(CHUNKS):
        part = pl.ds(q * block, block)
        hop(1, q).wait_recv()
        partial[side, level, part] = partial[side, level, part] + inbox[0, part]

        @pl.when(sends(2))
        def _():
            hop(2, q).start()

    far[0][0, pl.ds(pl.multiple_of(me * deep, SUB), deep), :] = series[LOCAL][me]
    for i in range(LEVELS - LOCAL):
        count = total >> (LOCAL + i)
        far[i][0, pl.ds(count, 2 * SUB), :] = jnp.zeros((2 * SUB, LANES), jnp.float32)

    @pl.loop(1, n)
    def _(d):
        spread(me, lax.rem(me + n - d, n)).wait_recv()

    lag = lax.broadcasted_iota(jnp.int32, (SUB, LANES), 0)

    def weight(l, h):
        return 1.0 / ((total >> l) - h * SUB - lag).astype(jnp.float32)

    for i in range(LEVELS - LOCAL):
        l = LOCAL + i
        count = total >> l
        if i > 0:
            far[i][0, pl.ds(0, count), :] = halve(far[i - 1], 0, 0, count)
        sums = add_lags(far[i], 0, range(count // SUB), [None] * LAGS)
        for h in range(LAGS // SUB):
            result[pl.ds(l * LAGS + h * SUB, SUB), :] = fold_rows(
                sums[h * SUB : (h + 1) * SUB]
            ) * weight(l, h)

    def deliver(peer, source):
        return pltpu.make_async_remote_copy(
            src_ref=result.at[pl.ds(pl.multiple_of(peer * rows_out, SUB), rows_out), :],
            dst_ref=out_ref.at[:, pl.ds(pl.multiple_of(source * LANES, LANES), LANES)],
            send_sem=out_send.at[peer],
            recv_sem=out_recv.at[source],
            device_id={"tm": peer},
            device_id_type=pl.DeviceIdType.MESH,
        )

    @pl.loop(1, n)
    def _(d):
        peer = lax.rem(me + d, n)

        @pl.when(peer >= keep)
        def _():
            deliver(peer, me).start()

    for s in range(2, len(stages)):

        @pl.when(receives(s))
        def _():
            for q in range(CHUNKS):
                part = pl.ds(q * block, block)
                hop(s, q).wait_recv()
                partial[side, level, part] = partial[side, level, part] + inbox[s - 1, part]
                if s + 1 < len(stages):

                    @pl.when(sends(s + 1))
                    def _():
                        hop(s + 1, q).start()

    @pl.when(me < keep)
    def _():
        count = total // (level + 1) - side * SUB
        scale = 1.0 / (count - lag).astype(jnp.float32)
        for c in range(n):
            out_ref[:, pl.ds(c * LANES, LANES)] = partial[side, level, c] * scale

    @pl.when(me >= keep)
    def _():
        out_ref[:, pl.ds(pl.multiple_of(me * LANES, LANES), LANES)] = result[
            pl.ds(pl.multiple_of(me * rows_out, SUB), rows_out), :
        ]

        @pl.loop(1, n)
        def _(d):
            deliver(me, lax.rem(me + n - d, n)).wait_recv()

    @pl.loop(1, n)
    def _(d):
        peer = lax.rem(me + n - d, n)
        spread(peer, me).wait_send()

        @pl.when(peer >= keep)
        def _():
            deliver(peer, me).wait_send()

    for q in range(CHUNKS):
        hop(0, q).wait_send()
        hop(1, q).wait_send()
    for s in range(2, len(stages)):

        @pl.when(sends(s))
        def _():
            for q in range(CHUNKS):
                hop(s, q).wait_send()

    @pl.when(me > 0)
    def _():
        for l in range(LOCAL):
            for q in range(CHUNKS):
                halo(l, q).wait_send()


def kernel_body(n, intensity, cycle_label, valid_mask):
    frames, pixels = intensity.shape
    f32 = jnp.float32
    dma = pltpu.SemaphoreType.DMA
    scratch = [
        pltpu.VMEM((frames, pixels), f32),
        pltpu.VMEM((pixels // 256, Q, 256), jnp.bfloat16),
    ]
    scratch += [pltpu.VMEM((n, (frames >> l) + 2 * SUB, LANES), f32) for l in range(LOCAL)]
    scratch += [pltpu.VMEM((n, frames >> LOCAL, LANES), f32)]
    scratch += [
        pltpu.VMEM((1, (n * frames >> l) + 2 * SUB, LANES), f32) for l in range(LOCAL, LEVELS)
    ]
    scratch += [
        pltpu.VMEM((n, LOCAL * LAGS, SUB, LANES), f32),
        pltpu.VMEM((2, 2, n, SUB, LANES), f32),
        pltpu.VMEM((2, n, SUB, LANES), f32),
        pltpu.VMEM((n.bit_length() - 2, n, SUB, LANES), f32),
        pltpu.VMEM((LEVELS * LAGS, LANES), f32),
        dma((pixels // 256,)),
        dma((LOCAL, CHUNKS)),
        dma((LOCAL, CHUNKS)),
        dma((n.bit_length() - 1, CHUNKS)),
        dma((n.bit_length() - 1, CHUNKS)),
    ] + [dma((n,))] * 4
    vmem = pl.BlockSpec(memory_space=pltpu.VMEM)
    return pl.pallas_call(
        functools.partial(kernel, n, frames),
        out_shape=jax.ShapeDtypeStruct((LEVELS * LAGS // n, pixels), f32),
        in_specs=[pl.BlockSpec(memory_space=pl.ANY), vmem, vmem],
        out_specs=vmem,
        scratch_shapes=scratch,
        compiler_params=pltpu.CompilerParams(collective_id=0, has_side_effects=True),
        name="multitau",
    )(intensity, cycle_label.reshape(1, pixels), valid_mask.reshape(1, pixels))


def route(intensity, cycle_label, valid_mask):
    n = lax.axis_size("tm")
    frames, pixels = intensity.shape
    fits = (
        lax.axis_size("pix") == 1
        and pixels == n * LANES
        and frames % (SUB << LOCAL) == 0
        and frames >> LOCAL >= 2 * SUB
        and LEVELS * LAGS == n * SUB
    )
    if fits:
        return kernel_body(n, intensity, cycle_label, valid_mask)
    return body(intensity, cycle_label, valid_mask)


def solution(mesh):
    placed = (P("tm", ("runs", "pix")), P(("runs", "pix")), P(("runs", "pix")))
    return jax.shard_map(
        route, mesh=mesh, in_specs=placed, out_specs=P("tm", ("runs", "pix")), check_vma=False
    )
```
